32 devices in a mesh: section: 8 (over z, y), tp: 4 (over x, core).
Axes of the slice: x: 2, y: 2, z: 4, core: 2. Of those that a mesh axis runs over, the one named last changes fastest.
Arguments:
- inputs: bfloat16 [8, 64, 4096], P('section', 'tp'), may hold values from -6 to 6
- hidden_grad: bfloat16 [8, 64, 14336], P('section', None, 'tp'), may hold values from -6 to 6
- top_grad: bfloat16 [64, 4096], P('tp'), may hold values from -6 to 6
- w_gate: bfloat16 [8, 96, 128, 128], P('section', 'tp'), may hold values from -0.5 to 0.5
- w_up: bfloat16 [8, 96, 128, 128], P('section', 'tp'), may hold values from -0.5 to 0.5
- block_pos: int32 [8, 96], P('section', 'tp'), may hold values from 0 to 895, as said below
- live_count: int32 [8, 4], P('section', 'tp'), may hold values from 6 to 24, as said below
Outputs:
- input_grad: bfloat16 [8, 64, 4096], P('section', 'tp')
- gate_wgrad: bfloat16 [8, 96, 128, 128], P('section', 'tp')
- up_wgrad: bfloat16 [8, 96, 128, 128], P('section', 'tp')
The draws below stay inside these ranges and needn't reach their ends.
Inputs may be any that keep to these rules, and one draw needn't show every extreme that they name: `block_pos`: within one layer and shard the 24 positions are distinct; p // 28 is the row block and p % 28 the column block. `live_count`: the live slots of a shard are its first ones; in every layer one shard has all 24 slots live.
All inputs are finite; a program needn't handle non-finite values.
Results may differ from the reference program's by a relative error of at most 0.0085.
Values may be sent and summed in bfloat16 or wider, within the bound.
No kernel may reach another device: no remote copies, remote signals or barrier semaphores. Data moves between devices by JAX's collectives and lax.ppermute only.
A program may use at most 64 MiB of HBM per device.

```python
import jax
import jax.numpy as jnp
from jax import lax

D = 4096
HIDDEN_UNITS = 14336
BLOCK_SIDE = 128
CAP = 24
ROWS = 64
SECTIONS = 8
POS = 896
N_TP = 4


def draw_block_pos(key, part):
    keys = jax.random.split(jax.random.fold_in(key, 11), SECTIONS * N_TP)
    chosen = jax.vmap(lambda single: jax.random.permutation(single, POS)[:CAP])(keys)
    return chosen.reshape(SECTIONS, N_TP * CAP).astype(jnp.int32)


def draw_live_count(key, part):
    first = jax.random.fold_in(key, 21)
    second = jax.random.fold_in(key, 22)
    base = jax.random.randint(first, (SECTIONS, N_TP), CAP // 4, CAP // 2 + 1)
    busiest = jax.random.randint(second, (SECTIONS,), 0, N_TP)
    shard_iota = jnp.arange(N_TP, dtype=jnp.int32)[None, :]
    return jnp.where(shard_iota == busiest[:, None], CAP, base).astype(jnp.int32)


def block_scale(key, extent, pieces, smallest, largest):
    def one(dim, parts):
        heights = jax.random.uniform(jax.random.fold_in(jax.random.fold_in(key, 6), dim), (parts,), jnp.float32, smallest / len(pieces), largest / len(pieces))
        return jnp.repeat(jnp.exp(heights), extent[dim] // parts).reshape((-1,) + (1,) * (len(extent) - dim - 1))

    factor_of = one(*pieces[0])
    for cut in pieces[1:]:
        factor_of = factor_of * one(*cut)
    return factor_of


def noise(rng, dims, deviation, bound, cuts=(), kind=jnp.bfloat16):
    drawn = deviation * jax.random.normal(rng, dims, jnp.float32)
    if cuts:
        drawn = drawn * block_scale(rng, dims, cuts, -0.22, 0.18)
    return jnp.clip(drawn, -bound, bound).astype(kind)


def setup_inputs(seed: int = 0) -> dict:
    splits = jax.random.split(jax.random.key(seed), 8)
    inputs = noise(splits[0], (SECTIONS, ROWS, D), 1.0, 6.0, ((0, 8), (1, 4)))
    hidden_grad = noise(splits[1], (SECTIONS, ROWS, HIDDEN_UNITS), 1.0, 6.0, ((0, 8), (2, 4)))
    top_grad = noise(splits[2], (ROWS, D), 1.0, 6.0, ((0, 4),))
    w_gate = noise(splits[3], (SECTIONS, N_TP * CAP, BLOCK_SIDE, BLOCK_SIDE), BLOCK_SIDE ** -0.5, 0.5, ((0, 8), (1, 4)))
    w_up = noise(splits[4], (SECTIONS, N_TP * CAP, BLOCK_SIDE, BLOCK_SIDE), BLOCK_SIDE ** -0.5, 0.5, ((0, 8), (1, 4)))
    block_pos = draw_block_pos(jax.random.fold_in(splits[7], 71), 0)
    live_count = draw_live_count(jax.random.fold_in(splits[7], 71), 0)
    return {"inputs": inputs, "hidden_grad": hidden_grad, "top_grad": top_grad, "w_gate": w_gate, "w_up": w_up, "block_pos": block_pos, "live_count": live_count}


def section_grads(args):
    rows_in, upstream, gate_weight_blocks, up_weight_blocks, position, block_counts = args
    single_float = jnp.float32
    highest_precision = lax.Precision.HIGHEST
    block_positions = N_TP * CAP
    col_blocks = HIDDEN_UNITS // (N_TP * BLOCK_SIDE)
    row_block_index = D // BLOCK_SIDE
    slot_iota = jnp.arange(block_positions, dtype=jnp.int32)
    device_part = slot_iota // CAP
    inside_block = slot_iota % CAP
    block_active_mask = (inside_block < block_counts[device_part]).astype(single_float)
    row_lookup = (position // col_blocks).astype(jnp.int32)
    column_lookup = (device_part * col_blocks + position % col_blocks).astype(jnp.int32)
    split = rows_in.astype(single_float).reshape(ROWS, row_block_index, BLOCK_SIDE)
    collected_rows = jnp.take(split, row_lookup, axis=1)
    wg = gate_weight_blocks.astype(single_float)
    wu = up_weight_blocks.astype(single_float)
    column_picker = (column_lookup[:, None] == jnp.arange(HIDDEN_UNITS // BLOCK_SIDE, dtype=jnp.int32)[None, :]).astype(single_float) * block_active_mask[:, None]
    pre_gate = jnp.einsum("rkd,kdn->krn", collected_rows, wg, precision=highest_precision)
    pre_up = jnp.einsum("rkd,kdn->krn", collected_rows, wu, precision=highest_precision)
    gate = jnp.einsum("kj,krn->rjn", column_picker, pre_gate, precision=highest_precision).reshape(ROWS, HIDDEN_UNITS)
    up = jnp.einsum("kj,krn->rjn", column_picker, pre_up, precision=highest_precision).reshape(ROWS, HIDDEN_UNITS)
    sig = jax.nn.sigmoid(gate)
    upstream_f = upstream.astype(single_float)
    dgate = (upstream_f * up * sig * (1.0 + gate * (1.0 - sig))).astype(jnp.bfloat16)
    dup = (upstream_f * gate * sig).astype(jnp.bfloat16)
    gate_gradient_columns = jnp.take(dgate.astype(single_float).reshape(ROWS, HIDDEN_UNITS // BLOCK_SIDE, BLOCK_SIDE), column_lookup, axis=1)
    up_gradient_columns = jnp.take(dup.astype(single_float).reshape(ROWS, HIDDEN_UNITS // BLOCK_SIDE, BLOCK_SIDE), column_lookup, axis=1)
    gate_gradient = jnp.einsum("vof,vow->ofw", collected_rows, gate_gradient_columns, precision=highest_precision) * block_active_mask[:, None, None]
    up_gradient = jnp.einsum("vof,vow->ofw", collected_rows, up_gradient_columns, precision=highest_precision) * block_active_mask[:, None, None]
    back_rows = jnp.einsum("rkn,kdn->krd", gate_gradient_columns, wg, precision=highest_precision) + jnp.einsum("rkn,kdn->krd", up_gradient_columns, wu, precision=highest_precision)
    row_picker = (row_lookup[:, None] == jnp.arange(row_block_index, dtype=jnp.int32)[None, :]).astype(single_float) * block_active_mask[:, None]
    per_shard = jnp.einsum("tkb,tkrd->trbd", row_picker.reshape(N_TP, CAP, row_block_index), back_rows.reshape(N_TP, CAP, ROWS, BLOCK_SIDE), precision=highest_precision)
    rounded = lax.optimization_barrier(per_shard.astype(jnp.bfloat16)).astype(single_float)
    contrib = jnp.sum(rounded, axis=0).reshape(ROWS, D)
    return contrib, gate_gradient.astype(jnp.bfloat16), up_gradient.astype(jnp.bfloat16)


def reference(inputs, hidden_grad, top_grad, w_gate, w_up, block_pos, live_count):
    contribs, gate_wgrad, up_wgrad = lax.map(section_grads, (inputs, hidden_grad, w_gate, w_up, block_pos, live_count))
    suffix = jnp.cumsum(contribs[::-1], axis=0)[::-1]
    input_grad = (suffix + top_grad.astype(jnp.float32)[None]).astype(jnp.bfloat16)
    return input_grad, gate_wgrad, up_wgrad
```

```python
import functools

import jax
import jax.numpy as jnp
from jax import lax
from jax.experimental import pallas as pl
from jax.experimental.pallas import tpu as pltpu
from jax.sharding import PartitionSpec as P

F32 = jnp.float32
BF16 = jnp.bfloat16


def _forward_back(
    masks, blk, table_ref, place_ref, *refs
):
    pieces, refs = refs[: len(masks)], refs[len(masks) :]
    grad_ref, wg_ref, wu_ref, x_ref, cot_ref, *rest = refs
    outs, (act_ref, back_ref) = rest[:-2], rest[-2:]
    slots = wg_ref.shape[0]
    rows = x_ref.shape[0]
    row_blocks = x_ref.shape[1] // blk
    col_blocks = cot_ref.shape[0] - 1
    me = place_ref[0]
    for mask, piece in zip(masks, pieces, strict=True):
        count = piece.shape[0]
        if count == rows:
            x_ref[...] = piece[...]
        else:
            start = pl.multiple_of((me ^ mask) * count, count)
            x_ref[pl.ds(start, count), :] = piece[...]
    act_ref[...] = jnp.zeros_like(act_ref)
    back_ref[...] = jnp.zeros_like(back_ref)

    def weights(slot):
        return jnp.concatenate([wg_ref[slot], wu_ref[slot]], axis=1)

    for slot in range(slots):
        start = pl.multiple_of(table_ref[0, slot] * blk, blk)
        pre = jnp.dot(x_ref[:, pl.ds(start, blk)], weights(slot), preferred_element_type=F32)
        act_ref[table_ref[1, slot]] += pre
    for col in range(col_blocks):
        gate = act_ref[col, :, :blk]
        up = act_ref[col, :, blk:]
        upstream = grad_ref[:, col * blk : (col + 1) * blk].astype(F32)
        sig = jax.nn.sigmoid(gate)
        scaled = upstream * sig
        cot_ref[col, :, :blk] = (scaled * up * (1.0 + gate * (1.0 - sig))).astype(BF16)
        cot_ref[col, :, blk:] = (scaled * gate).astype(BF16)
    cot_ref[col_blocks] = jnp.zeros_like(cot_ref[col_blocks])
    for slot in range(slots):
        back = lax.dot_general(
            cot_ref[table_ref[1, slot]],
            weights(slot),
            (((1,), (1,)), ((), ())),
            preferred_element_type=F32,
        )
        back_ref[table_ref[0, slot]] += back
    if len(masks) == 1:
        for row in range(row_blocks):
            outs[0][:, row * blk : (row + 1) * blk] = back_ref[row].astype(BF16)
        return
    count = rows // len(masks)
    keep_ref, far_ref, send_ref = outs
    for target, mask in (
        (keep_ref, 0),
        (far_ref, 2),
        (send_ref.at[0], 1),
        (send_ref.at[1], 3),
    ):
        start = pl.multiple_of((me ^ mask) * count, count)
        for row in range(row_blocks):
            target[:, row * blk : (row + 1) * blk] = back_ref[row, pl.ds(start, count), :].astype(
                target.dtype
            )


def _weight_grads(blk, table_ref, x_ref, cot_ref, gate_ref, up_ref):
    slots = gate_ref.shape[0]
    for slot in range(slots):
        start = pl.multiple_of(table_ref[0, slot] * blk, blk)
        grads = lax.dot_general(
            x_ref[:, pl.ds(start, blk)],
            cot_ref[table_ref[1, slot]],
            (((0,), (0,)), ((), ())),
            preferred_element_type=F32,
        )
        gate_ref[slot] = grads[:, :blk].astype(BF16)
        up_ref[slot] = grads[:, blk:].astype(BF16)


def _swap(array, axis, distance):
    count = lax.axis_size(axis)
    return lax.ppermute(array, axis, [(i, i ^ distance) for i in range(count)])


def local(inputs, hidden_grad, top_grad, w_gate, w_up, block_pos, live_count):
    own_rows = inputs[0]
    count, width = own_rows.shape
    slots, blk = w_gate.shape[1], w_gate.shape[2]
    col_blocks = hidden_grad.shape[2] // blk
    tp = lax.axis_size("tp")
    sections = lax.axis_size("section")
    rows = count * tp
    me = lax.axis_index("tp")
    section = lax.axis_index("section")

    position = block_pos[0]
    live = lax.iota(jnp.int32, slots) < live_count[0, 0]
    table = jnp.stack(
        [position // col_blocks, jnp.where(live, position % col_blocks, col_blocks)]
    )
    place = jnp.reshape(me, (1,)).astype(jnp.int32)

    paired = tp == 4
    if paired:
        across = _swap(own_rows, "tp", 2)
        beside = _swap(own_rows, "tp", 1)
        beyond = _swap(across, "tp", 1)
        pieces, masks = (own_rows, beside, across, beyond), (0, 1, 2, 3)
        terms = (
            jax.ShapeDtypeStruct((count, width), F32),
            jax.ShapeDtypeStruct((count, width), F32),
            jax.ShapeDtypeStruct((2, count, width), BF16),
        )
    else:
        pieces, masks = (lax.all_gather(own_rows, "tp", axis=0, tiled=True),), (0,)
        terms = (jax.ShapeDtypeStruct((rows, width), BF16),)

    vmem = pl.BlockSpec(memory_space=pltpu.VMEM)
    smem = pl.BlockSpec(memory_space=pltpu.SMEM)
    x_all, cot, *terms = pl.pallas_call(
        functools.partial(_forward_back, masks, blk),
        out_shape=(
            jax.ShapeDtypeStruct((rows, width), BF16),
            jax.ShapeDtypeStruct((col_blocks + 1, rows, 2 * blk), BF16),
            *terms,
        ),
        in_specs=[smem, smem] + [vmem] * (len(pieces) + 3),
        out_specs=[vmem] * (2 + len(terms)),
        scratch_shapes=[
            pltpu.VMEM((col_blocks + 1, rows, 2 * blk), F32),
            pltpu.VMEM((width // blk, rows, blk), F32),
        ],
        compiler_params=pltpu.CompilerParams(vmem_limit_bytes=48 << 20),
        name="forward_back",
    )(table, place, *pieces, hidden_grad[0], w_gate[0], w_up[0])

    gate_gradient, up_gradient = pl.pallas_call(
        functools.partial(_weight_grads, blk),
        out_shape=(jax.ShapeDtypeStruct((slots, blk, blk), BF16),) * 2,
        in_specs=[smem, vmem, vmem],
        out_specs=[vmem, vmem],
        compiler_params=pltpu.CompilerParams(vmem_limit_bytes=48 << 20),
        name="weight_grads",
    )(table, x_all, cot)

    if paired:
        keep, far, send = terms
        came = _swap(send, "tp", 1)
        crossed = _swap((far + came[1].astype(F32)).astype(BF16), "tp", 2)
        own_term = keep + came[0].astype(F32) + crossed.astype(F32)
    else:
        own_term = lax.psum_scatter(terms[0], "tp", scatter_dimension=0, tiled=True).astype(F32)

    total = own_term
    result = top_grad.astype(F32) + own_term
    if sections & (sections - 1) == 0:
        distance = 1
        while distance < sections:
            other = _swap(total.astype(BF16), "section", distance).astype(F32)
            result = result + jnp.where(section & distance == 0, other, 0.0)
            total = total + other
            distance *= 2
    else:
        distance = 1
        while distance < sections:
            moves = [(i, i - distance) for i in range(distance, sections)]
            total = total + lax.ppermute(total.astype(BF16), "section", moves).astype(F32)
            distance *= 2
        result = top_grad.astype(F32) + total
    return (
        result.astype(BF16)[None],
        gate_gradient[None],
        up_gradient[None],
    )


def solution(mesh):
    in_specs = (
        P("section", "tp", None),
        P("section", None, "tp"),
        P("tp", None),
        P("section", "tp", None, None),
        P("section", "tp", None, None),
        P("section", "tp"),
        P("section", "tp"),
    )
    out_specs = (
        P("section", "tp", None),
        P("section", "tp", None, None),
        P("section", "tp", None, None),
    )
    return jax.shard_map(local, mesh=mesh, in_specs=in_specs, out_specs=out_specs, check_vma=False)
```

```python
import functools

import jax
import jax.numpy as jnp
from jax import lax
from jax.experimental import pallas as pl
from jax.experimental.pallas import tpu as pltpu
from jax.sharding import PartitionSpec as P

F32 = jnp.float32
BF16 = jnp.bfloat16


def _stage(own_in, grad_in, wg_in, wu_in, own_ref, grad_ref, weight_ref, sems):
    blk = wg_in.shape[2]
    copies = [
        pltpu.make_async_copy(wg_in, weight_ref.at[:, :, :blk], sems.at[0]),
        pltpu.make_async_copy(wu_in, weight_ref.at[:, :, blk:], sems.at[1]),
        pltpu.make_async_copy(grad_in, grad_ref, sems.at[2]),
        pltpu.make_async_copy(own_in, own_ref, sems.at[3]),
    ]
    for copy in copies:
        copy.start()
    for copy in copies:
        copy.wait()


def _forward_back(masks, blk, table_ref, place_ref, *refs):
    pieces, refs = refs[: len(masks)], refs[len(masks) :]
    grad_ref, weight_ref, x_ref, cot_ref, *rest = refs
    outs, (act_ref, back_ref) = rest[:-2], rest[-2:]
    slots = weight_ref.shape[0]
    rows = x_ref.shape[0]
    row_blocks = x_ref.shape[1] // blk
    col_blocks = cot_ref.shape[0] - 1
    me = place_ref[0]
    for mask, piece in zip(masks, pieces, strict=True):
        count = piece.shape[0]
        if count == rows:
            x_ref[...] = piece[...]
        else:
            start = pl.multiple_of((me ^ mask) * count, count)
            x_ref[pl.ds(start, count), :] = piece[...]
    act_ref[...] = jnp.zeros_like(act_ref)
    back_ref[...] = jnp.zeros_like(back_ref)

    for slot in range(slots):
        start = pl.multiple_of(table_ref[0, slot] * blk, blk)
        pre = jnp.dot(x_ref[:, pl.ds(start, blk)], weight_ref[slot], preferred_element_type=F32)
        act_ref[table_ref[1, slot]] += pre
    for col in range(col_blocks):
        gate = act_ref[col, :, :blk]
        up = act_ref[col, :, blk:]
        upstream = grad_ref[:, col * blk : (col + 1) * blk].astype(F32)
        sig = jax.nn.sigmoid(gate)
        scaled = upstream * sig
        cot_ref[col, :, :blk] = (scaled * up * (1.0 + gate * (1.0 - sig))).astype(BF16)
        cot_ref[col, :, blk:] = (scaled * gate).astype(BF16)
    cot_ref[col_blocks] = jnp.zeros_like(cot_ref[col_blocks])
    for slot in range(slots):
        back = lax.dot_general(
            cot_ref[table_ref[1, slot]],
            weight_ref[slot],
            (((1,), (1,)), ((), ())),
            preferred_element_type=F32,
        )
        back_ref[table_ref[0, slot]] += back
    if len(masks) == 1:
        for row in range(row_blocks):
            outs[0][:, row * blk : (row + 1) * blk] = back_ref[row].astype(BF16)
        return
    count = rows // len(masks)
    keep_ref, far_ref, send_ref = outs
    for target, mask in (
        (keep_ref, 0),
        (far_ref, 2),
        (send_ref.at[0], 1),
        (send_ref.at[1], 3),
    ):
        start = pl.multiple_of((me ^ mask) * count, count)
        for row in range(row_blocks):
            target[:, row * blk : (row + 1) * blk] = back_ref[row, pl.ds(start, count), :].astype(
                target.dtype
            )


def _weight_grads(blk, table_ref, x_ref, cot_ref, gate_ref, up_ref):
    slots = gate_ref.shape[0]
    for slot in range(slots):
        start = pl.multiple_of(table_ref[0, slot] * blk, blk)
        grads = lax.dot_general(
            x_ref[:, pl.ds(start, blk)],
            cot_ref[table_ref[1, slot]],
            (((0,), (0,)), ((), ())),
            preferred_element_type=F32,
        )
        gate_ref[slot] = grads[:, :blk].astype(BF16)
        up_ref[slot] = grads[:, blk:].astype(BF16)


_pinned = pltpu.with_memory_space_constraint


def _swap(array, axis, distance):
    count = lax.axis_size(axis)
    return lax.ppermute(array, axis, [(i, i ^ distance) for i in range(count)])


def local(inputs, hidden_grad, top_grad, w_gate, w_up, block_pos, live_count):
    own_rows = inputs[0]
    count, width = own_rows.shape
    slots, blk = w_gate.shape[1], w_gate.shape[2]
    col_blocks = hidden_grad.shape[2] // blk
    tp = lax.axis_size("tp")
    sections = lax.axis_size("section")
    rows = count * tp
    me = lax.axis_index("tp")
    section = lax.axis_index("section")

    position = block_pos[0]
    live = lax.iota(jnp.int32, slots) < live_count[0, 0]
    table = jnp.stack(
        [position // col_blocks, jnp.where(live, position % col_blocks, col_blocks)]
    )
    place = jnp.reshape(me, (1,)).astype(jnp.int32)

    vmem = pl.BlockSpec(memory_space=pltpu.VMEM)
    smem = pl.BlockSpec(memory_space=pltpu.SMEM)
    own_staged, grad_staged, weights = pl.pallas_call(
        _stage,
        out_shape=(
            jax.ShapeDtypeStruct(own_rows.shape, BF16),
            jax.ShapeDtypeStruct(hidden_grad.shape[1:], BF16),
            jax.ShapeDtypeStruct((slots, blk, 2 * blk), BF16),
        ),
        in_specs=[pl.BlockSpec(memory_space=pltpu.HBM)] * 4,
        out_specs=[vmem] * 3,
        scratch_shapes=[pltpu.SemaphoreType.DMA((4,))],
        compiler_params=pltpu.CompilerParams(vmem_limit_bytes=4 << 20),
        name="stage",
    )(*(_pinned(array, pltpu.HBM) for array in (own_rows, hidden_grad[0], w_gate[0], w_up[0])))

    paired = tp == 4
    if paired:
        across = _swap(own_rows, "tp", 2)
        beside = _swap(own_rows, "tp", 1)
        beyond = _swap(across, "tp", 1)
        pieces, masks = (own_staged, beside, across, beyond), (0, 1, 2, 3)
        terms = (
            jax.ShapeDtypeStruct((count, width), F32),
            jax.ShapeDtypeStruct((count, width), F32),
            jax.ShapeDtypeStruct((2, count, width), BF16),
        )
    else:
        pieces, masks = (lax.all_gather(own_rows, "tp", axis=0, tiled=True),), (0,)
        terms = (jax.ShapeDtypeStruct((rows, width), BF16),)

    x_all, cot, *terms = pl.pallas_call(
        functools.partial(_forward_back, masks, blk),
        out_shape=(
            jax.ShapeDtypeStruct((rows, width), BF16),
            jax.ShapeDtypeStruct((col_blocks + 1, rows, 2 * blk), BF16),
            *terms,
        ),
        in_specs=[smem, smem] + [vmem] * (len(pieces) + 2),
        out_specs=[vmem] * (2 + len(terms)),
        scratch_shapes=[
            pltpu.VMEM((col_blocks + 1, rows, 2 * blk), F32),
            pltpu.VMEM((width // blk, rows, blk), F32),
        ],
        compiler_params=pltpu.CompilerParams(vmem_limit_bytes=12 << 20),
        name="forward_back",
    )(table, place, *(_pinned(array, pltpu.VMEM) for array in (*pieces, grad_staged, weights)))

    gate_gradient, up_gradient = pl.pallas_call(
        functools.partial(_weight_grads, blk),
        out_shape=(jax.ShapeDtypeStruct((slots, blk, blk), BF16),) * 2,
        in_specs=[smem, vmem, vmem],
        out_specs=[vmem, vmem],
        compiler_params=pltpu.CompilerParams(vmem_limit_bytes=8 << 20),
        name="weight_grads",
    )(table, x_all, cot)

    if paired:
        keep, far, send = terms
        came = _swap(send, "tp", 1)
        crossed = _swap((far + came[1].astype(F32)).astype(BF16), "tp", 2)
        own_term = keep + came[0].astype(F32) + crossed.astype(F32)
    else:
        own_term = lax.psum_scatter(terms[0], "tp", scatter_dimension=0, tiled=True).astype(F32)

    total = own_term
    result = top_grad.astype(F32) + own_term
    if sections & (sections - 1) == 0:
        block = min(sections, 4)
        sent = own_term.astype(BF16)
        for step in range(1, block):
            other = _swap(sent, "section", step).astype(F32)
            result = result + jnp.where((section ^ step) > section, other, 0.0)
            total = total + other
        while block < sections:
            other = _swap(total.astype(BF16), "section", block ^ (block >> 1)).astype(F32)
            result = result + jnp.where(section & block == 0, other, 0.0)
            total = total + other
            block *= 2
    else:
        distance = 1
        while distance < sections:
            moves = [(i, i - distance) for i in range(distance, sections)]
            total = total + lax.ppermute(total.astype(BF16), "section", moves).astype(F32)
            distance *= 2
        result = top_grad.astype(F32) + total
    return (
        result.astype(BF16)[None],
        gate_gradient[None],
        up_gradient[None],
    )


def solution(mesh):
    in_specs = (
        P("section", "tp", None),
        P("section", None, "tp"),
        P("tp", None),
        P("section", "tp", None, None),
        P("section", "tp", None, None),
        P("section", "tp"),
        P("section", "tp"),
    )
    out_specs = (
        P("section", "tp", None),
        P("section", "tp", None, None),
        P("section", "tp", None, None),
    )
    return jax.shard_map(local, mesh=mesh, in_specs=in_specs, out_specs=out_specs, check_vma=False)
```

```python
import functools

import jax
import jax.numpy as jnp
from jax import lax
from jax.experimental import pallas as pl
from jax.experimental.pallas import tpu as pltpu
from jax.sharding import PartitionSpec as P

F32 = jnp.float32
BF16 = jnp.bfloat16
PARTS = 4


def _shift_and_factor(divisor, limit):
    for shift in range(31):
        factor = -(-(1 << shift) // divisor)
        if factor * limit < 1 << 31 and all(
            (p * factor) >> shift == p // divisor for p in range(limit)
        ):
            return factor, shift
    raise ValueError(divisor)


def _slot(position_ref, live_ref, slot, col_blocks, row_blocks):
    factor, shift = _shift_and_factor(col_blocks, col_blocks * row_blocks)
    position = position_ref[0, slot]
    row = (position * factor) >> shift
    col = position - row * col_blocks
    return row, jnp.where(slot < live_ref[0, 0], col, col_blocks)


def _term(blk, table, grad, weight_ref, ready, x_ref, cot_ref, act_ref, back_ref):
    col_blocks = cot_ref.shape[0] - 1
    slots = len(table)
    for slot, (row, col) in enumerate(table):
        ready(slot)
        start = pl.multiple_of(row * blk, blk)
        act_ref[col] += jnp.dot(
            x_ref[:, pl.ds(start, blk)], weight_ref[slot], preferred_element_type=F32
        )
    for col in range(col_blocks):
        gate = act_ref[col, :, :blk]
        up = act_ref[col, :, blk:]
        upstream = grad(col).astype(F32)
        sig = jax.nn.sigmoid(gate)
        scaled = upstream * sig
        cot_ref[col, :, :blk] = (scaled * up * (1.0 + gate * (1.0 - sig))).astype(BF16)
        cot_ref[col, :, blk:] = (scaled * gate).astype(BF16)
    cot_ref[col_blocks] = jnp.zeros_like(cot_ref[col_blocks])
    for slot in range(slots):
        row, col = table[slot]
        back_ref[row] += lax.dot_general(
            cot_ref[col], weight_ref[slot], (((1,), (1,)), ((), ())), preferred_element_type=F32
        )


def _write_rows(back_ref, start, count, target):
    blk = back_ref.shape[2]
    for row in range(back_ref.shape[0]):
        target[:, row * blk : (row + 1) * blk] = back_ref[row, pl.ds(start, count), :].astype(
            target.dtype
        )


def _near_half(
    blk,
    position_ref,
    live_ref,
    own_in,
    beside_ref,
    grad_in,
    wg_in,
    wu_in,
    x_ref,
    cot_ref,
    keep_ref,
    send_ref,
    weight_ref,
    far_grad_ref,
    grad_ref,
    act_ref,
    back_ref,
    sems,
):
    me = lax.axis_index("tp")
    core, chip = me & 1, me >> 1
    count = own_in.shape[0]
    slots = wg_in.shape[0]
    part = slots // PARTS
    rows = 2 * count
    mine = pl.multiple_of(core * count, count)
    other = pl.multiple_of((core ^ 1) * count, count)
    near = pl.multiple_of(chip * rows, rows)
    far = pl.multiple_of((chip ^ 1) * rows, rows)
    own = pltpu.make_async_copy(own_in, x_ref.at[pl.ds(mine, count), :], sems.at[0])
    near_grad = pltpu.make_async_copy(grad_in.at[pl.ds(near, rows), :], grad_ref, sems.at[1])
    far_grad = pltpu.make_async_copy(grad_in.at[pl.ds(far, rows), :], far_grad_ref, sems.at[2])
    blocks = []
    for index in range(PARTS):
        span = pl.ds(index * part, part)
        blocks.append(
            [
                pltpu.make_async_copy(
                    wg_in.at[span], weight_ref.at[span, :, pl.ds(0, blk)], sems.at[3 + 2 * index]
                ),
                pltpu.make_async_copy(
                    wu_in.at[span], weight_ref.at[span, :, pl.ds(blk, blk)], sems.at[4 + 2 * index]
                ),
            ]
        )
    for copy in (own, *blocks[0], near_grad, *sum(blocks[1:], []), far_grad):
        copy.start()
    x_ref[pl.ds(other, count), :] = beside_ref[...]
    act_ref[...] = jnp.zeros_like(act_ref)
    back_ref[...] = jnp.zeros_like(back_ref)
    own.wait()
    table = [
        _slot(position_ref, live_ref, slot, cot_ref.shape[0] - 1, back_ref.shape[0])
        for slot in range(slots)
    ]

    def ready(slot):
        if slot % part == 0:
            for copy in blocks[slot // part]:
                copy.wait()

    def grad(col):
        if col == 0:
            near_grad.wait()
        return grad_ref[:, col * blk : (col + 1) * blk]

    _term(blk, table, grad, weight_ref, ready, x_ref, cot_ref, act_ref, back_ref)
    _write_rows(back_ref, mine, count, keep_ref)
    _write_rows(back_ref, other, count, send_ref)
    far_grad.wait()


def _far_half(
    blk,
    position_ref,
    live_ref,
    across_ref,
    beyond_ref,
    grad_ref,
    weight_ref,
    x_ref,
    cot_ref,
    far_ref,
    send_ref,
    act_ref,
    back_ref,
):
    me = lax.axis_index("tp")
    core = me & 1
    count = across_ref.shape[0]
    mine = pl.multiple_of(core * count, count)
    other = pl.multiple_of((core ^ 1) * count, count)
    x_ref[pl.ds(mine, count), :] = across_ref[...]
    x_ref[pl.ds(other, count), :] = beyond_ref[...]
    act_ref[...] = jnp.zeros_like(act_ref)
    back_ref[...] = jnp.zeros_like(back_ref)
    table = [
        _slot(position_ref, live_ref, slot, cot_ref.shape[0] - 1, back_ref.shape[0])
        for slot in range(weight_ref.shape[0])
    ]

    def grad(col):
        return grad_ref[:, col * blk : (col + 1) * blk]

    _term(blk, table, grad, weight_ref, lambda slot: None, x_ref, cot_ref, act_ref, back_ref)
    _write_rows(back_ref, other, count, send_ref)
    _write_rows(back_ref, mine, count, far_ref)


def _whole(
    blk,
    position_ref,
    live_ref,
    x_ref,
    grad_ref,
    wg_ref,
    wu_ref,
    cot_ref,
    term_ref,
    weight_ref,
    act_ref,
    back_ref,
):
    weight_ref[:, :, :blk] = wg_ref[...]
    weight_ref[:, :, blk:] = wu_ref[...]
    act_ref[...] = jnp.zeros_like(act_ref)
    back_ref[...] = jnp.zeros_like(back_ref)
    table = [
        _slot(position_ref, live_ref, slot, cot_ref.shape[0] - 1, back_ref.shape[0])
        for slot in range(weight_ref.shape[0])
    ]

    def grad(col):
        return grad_ref[:, col * blk : (col + 1) * blk]

    _term(blk, table, grad, weight_ref, lambda slot: None, x_ref, cot_ref, act_ref, back_ref)
    _write_rows(back_ref, 0, x_ref.shape[0], term_ref)


def _weight_grads(blk, halves, position_ref, live_ref, *refs):
    x_refs, cot_refs, (gate_ref, up_ref) = refs[:halves], refs[halves : 2 * halves], refs[-2:]
    for slot in range(gate_ref.shape[0]):
        row, col = _slot(
            position_ref, live_ref, slot, cot_refs[0].shape[0] - 1, x_refs[0].shape[1] // blk
        )
        start = pl.multiple_of(row * blk, blk)
        grads = lax.dot_general(
            jnp.concatenate([x_ref[:, pl.ds(start, blk)] for x_ref in x_refs], axis=0),
            jnp.concatenate([cot_ref[col] for cot_ref in cot_refs], axis=0),
            (((0,), (0,)), ((), ())),
            preferred_element_type=F32,
        )
        gate_ref[slot] = grads[:, :blk].astype(BF16)
        up_ref[slot] = grads[:, blk:].astype(BF16)


_pinned = pltpu.with_memory_space_constraint


def _swap(array, axis, distance):
    count = lax.axis_size(axis)
    return lax.ppermute(array, axis, [(i, i ^ distance) for i in range(count)])


def _params(mib):
    return pltpu.CompilerParams(vmem_limit_bytes=mib << 20)


def local(inputs, hidden_grad, top_grad, w_gate, w_up, block_pos, live_count):
    own_rows = inputs[0]
    count, width = own_rows.shape
    slots, blk = w_gate.shape[1], w_gate.shape[2]
    hidden = hidden_grad.shape[2]
    col_blocks, row_blocks = hidden // blk, width // blk
    tp = lax.axis_size("tp")
    sections = lax.axis_size("section")
    section = lax.axis_index("section")

    vmem = pl.BlockSpec(memory_space=pltpu.VMEM)
    smem = pl.BlockSpec(memory_space=pltpu.SMEM)
    hbm = pl.BlockSpec(memory_space=pltpu.HBM)
    struct = jax.ShapeDtypeStruct

    def cots(rows):
        return struct((col_blocks + 1, rows, 2 * blk), BF16)

    def sums(rows):
        return [
            pltpu.VMEM((col_blocks + 1, rows, 2 * blk), F32),
            pltpu.VMEM((row_blocks, rows, blk), F32),
        ]

    if tp == 4 and slots % PARTS == 0:
        rows = 2 * count
        across = _swap(own_rows, "tp", 2)
        beside = _swap(own_rows, "tp", 1)
        near_x, near_cot, keep, near_send, weights, far_grad = pl.pallas_call(
            functools.partial(_near_half, blk),
            out_shape=(
                struct((rows, width), BF16),
                cots(rows),
                struct((count, width), F32),
                struct((count, width), BF16),
                struct((slots, blk, 2 * blk), BF16),
                struct((rows, hidden), BF16),
            ),
            in_specs=[smem, smem, hbm, vmem, hbm, hbm, hbm],
            out_specs=[vmem] * 6,
            scratch_shapes=[
                pltpu.VMEM((rows, hidden), BF16),
                *sums(rows),
                pltpu.SemaphoreType.DMA((3 + 2 * PARTS,)),
            ],
            compiler_params=_params(10),
            name="near_half",
        )(
            block_pos,
            live_count,
            _pinned(own_rows, pltpu.HBM),
            beside,
            *(_pinned(array[0], pltpu.HBM) for array in (hidden_grad, w_gate, w_up)),
        )
        across, near_send = lax.optimization_barrier((across, near_send))
        beyond = _swap(across, "tp", 1)
        far_x, far_cot, far, far_send = pl.pallas_call(
            functools.partial(_far_half, blk),
            out_shape=(
                struct((rows, width), BF16),
                cots(rows),
                struct((count, width), F32),
                struct((count, width), BF16),
            ),
            in_specs=[smem, smem] + [vmem] * 4,
            out_specs=[vmem] * 4,
            scratch_shapes=sums(rows),
            compiler_params=_params(10),
            name="far_half",
        )(block_pos, live_count, across, beyond, far_grad, weights)
        near_came = _swap(near_send, "tp", 1)
        far_came = _swap(far_send, "tp", 1)
        crossed = _swap((far + far_came.astype(F32)).astype(BF16), "tp", 2)
        own_term = keep + near_came.astype(F32) + crossed.astype(F32)
        x_parts, cot_parts = (near_x, far_x), (near_cot, far_cot)
    else:
        rows = tp * count
        gathered = lax.all_gather(own_rows, "tp", axis=0, tiled=True)
        cot, term = pl.pallas_call(
            functools.partial(_whole, blk),
            out_shape=(cots(rows), struct((rows, width), BF16)),
            in_specs=[smem, smem] + [vmem] * 4,
            out_specs=[vmem] * 2,
            scratch_shapes=[pltpu.VMEM((slots, blk, 2 * blk), BF16), *sums(rows)],
            compiler_params=_params(24),
            name="whole",
        )(block_pos, live_count, gathered, hidden_grad[0], w_gate[0], w_up[0])
        own_term = lax.psum_scatter(term, "tp", scatter_dimension=0, tiled=True).astype(F32)
        x_parts, cot_parts = (gathered,), (cot,)

    gate_gradient, up_gradient = pl.pallas_call(
        functools.partial(_weight_grads, blk, len(x_parts)),
        out_shape=(struct((slots, blk, blk), BF16),) * 2,
        in_specs=[smem, smem] + [vmem] * (2 * len(x_parts)),
        out_specs=[vmem, vmem],
        compiler_params=_params(8),
        name="weight_grads",
    )(block_pos, live_count, *x_parts, *cot_parts)

    total = own_term
    result = top_grad.astype(F32) + own_term
    if sections & (sections - 1) == 0:
        block = min(sections, 4)
        sent = own_term.astype(BF16)
        for step in range(1, block):
            other = _swap(sent, "section", step).astype(F32)
            result = result + jnp.where((section ^ step) > section, other, 0.0)
            total = total + other
        while block < sections:
            other = _swap(total.astype(BF16), "section", block ^ (block >> 1)).astype(F32)
            result = result + jnp.where(section & block == 0, other, 0.0)
            total = total + other
            block *= 2
    else:
        distance = 1
        while distance < sections:
            moves = [(i, i - distance) for i in range(distance, sections)]
            total = total + lax.ppermute(total.astype(BF16), "section", moves).astype(F32)
            distance *= 2
        result = top_grad.astype(F32) + total
    return (
        result.astype(BF16)[None],
        gate_gradient[None],
        up_gradient[None],
    )


def solution(mesh):
    in_specs = (
        P("section", "tp", None),
        P("section", None, "tp"),
        P("tp", None),
        P("section", "tp", None, None),
        P("section", "tp", None, None),
        P("section", "tp"),
        P("section", "tp"),
    )
    out_specs = (
        P("section", "tp", None),
        P("section", "tp", None, None),
        P("section", "tp", None, None),
    )
    return jax.shard_map(local, mesh=mesh, in_specs=in_specs, out_specs=out_specs, check_vma=False)
```

```python
import functools

import jax
import jax.numpy as jnp
from jax import lax
from jax.experimental import pallas as pl
from jax.experimental.pallas import tpu as pltpu
from jax.sharding import PartitionSpec as P

F32 = jnp.float32
BF16 = jnp.bfloat16
PARTS = 4


def _shift_and_factor(divisor, limit):
    for shift in range(31):
        factor = -(-(1 << shift) // divisor)
        if factor * limit < 1 << 31 and all(
            (p * factor) >> shift == p // divisor for p in range(limit)
        ):
            return factor, shift
    raise ValueError(divisor)


def _make_table(position, live, col_blocks, row_blocks, table_ref):
    factor, shift = _shift_and_factor(col_blocks, col_blocks * row_blocks)
    row = (position * factor) >> shift
    slot = lax.broadcasted_iota(jnp.int32, position.shape, 1)
    table_ref[0:1, :] = row
    table_ref[1:2, :] = jnp.where(slot < live, position - row * col_blocks, col_blocks)


def _read_table(table_ref):
    table = table_ref[...]
    return [(table[0, slot], table[1, slot]) for slot in range(table.shape[1])]


def _term(blk, table, grad, weight_ref, ready, x_ref, cot_ref, act_ref, back_ref):
    col_blocks = cot_ref.shape[0] - 1
    slots = len(table)
    for slot, (row, col) in enumerate(table):
        ready(slot)
        start = pl.multiple_of(row * blk, blk)
        act_ref[col] += jnp.dot(
            x_ref[:, pl.ds(start, blk)], weight_ref[slot], preferred_element_type=F32
        )
    for col in range(col_blocks):
        gate = act_ref[col, :, :blk]
        up = act_ref[col, :, blk:]
        upstream = grad(col).astype(F32)
        sig = jax.nn.sigmoid(gate)
        scaled = upstream * sig
        cot_ref[col, :, :blk] = (scaled * up * (1.0 + gate * (1.0 - sig))).astype(BF16)
        cot_ref[col, :, blk:] = (scaled * gate).astype(BF16)
    cot_ref[col_blocks] = jnp.zeros_like(cot_ref[col_blocks])
    for slot in range(slots):
        row, col = table[slot]
        back_ref[row] += lax.dot_general(
            cot_ref[col], weight_ref[slot], (((1,), (1,)), ((), ())), preferred_element_type=F32
        )


def _write_rows(back_ref, start, count, target):
    blk = back_ref.shape[2]
    for row in range(back_ref.shape[0]):
        target[:, row * blk : (row + 1) * blk] = back_ref[row, pl.ds(start, count), :].astype(
            target.dtype
        )


def _near_half(
    blk,
    position_in,
    live_ref,
    own_in,
    beside_ref,
    grad_in,
    wg_in,
    wu_in,
    x_ref,
    cot_ref,
    keep_ref,
    send_ref,
    weight_ref,
    far_grad_ref,
    table_ref,
    position_ref,
    grad_ref,
    act_ref,
    back_ref,
    sems,
):
    me = lax.axis_index("tp")
    core, chip = me & 1, me >> 1
    count = own_in.shape[0]
    slots = wg_in.shape[0]
    part = slots // PARTS
    rows = 2 * count
    mine = pl.multiple_of(core * count, count)
    other = pl.multiple_of((core ^ 1) * count, count)
    near = pl.multiple_of(chip * rows, rows)
    far = pl.multiple_of((chip ^ 1) * rows, rows)
    position = pltpu.make_async_copy(position_in, position_ref, sems.at[3 + 2 * PARTS])
    own = pltpu.make_async_copy(own_in, x_ref.at[pl.ds(mine, count), :], sems.at[0])
    near_grad = pltpu.make_async_copy(grad_in.at[pl.ds(near, rows), :], grad_ref, sems.at[1])
    far_grad = pltpu.make_async_copy(grad_in.at[pl.ds(far, rows), :], far_grad_ref, sems.at[2])
    blocks = []
    for index in range(PARTS):
        span = pl.ds(index * part, part)
        blocks.append(
            [
                pltpu.make_async_copy(
                    wg_in.at[span], weight_ref.at[span, :, pl.ds(0, blk)], sems.at[3 + 2 * index]
                ),
                pltpu.make_async_copy(
                    wu_in.at[span], weight_ref.at[span, :, pl.ds(blk, blk)], sems.at[4 + 2 * index]
                ),
            ]
        )
    for copy in (position, own, *blocks[0], near_grad, *sum(blocks[1:], []), far_grad):
        copy.start()
    x_ref[pl.ds(other, count), :] = beside_ref[...]
    act_ref[...] = jnp.zeros_like(act_ref)
    back_ref[...] = jnp.zeros_like(back_ref)
    for copy in (position, own):
        copy.wait()
    _make_table(
        position_ref[...], live_ref[0, 0], cot_ref.shape[0] - 1, back_ref.shape[0], table_ref
    )
    table = _read_table(table_ref)

    def ready(slot):
        if slot % part == 0:
            for copy in blocks[slot // part]:
                copy.wait()

    def grad(col):
        if col == 0:
            near_grad.wait()
        return grad_ref[:, col * blk : (col + 1) * blk]

    _term(blk, table, grad, weight_ref, ready, x_ref, cot_ref, act_ref, back_ref)
    _write_rows(back_ref, mine, count, keep_ref)
    _write_rows(back_ref, other, count, send_ref)
    far_grad.wait()


def _far_half(
    blk,
    table_ref,
    across_ref,
    beyond_ref,
    grad_ref,
    weight_ref,
    x_ref,
    cot_ref,
    far_ref,
    send_ref,
    act_ref,
    back_ref,
):
    me = lax.axis_index("tp")
    core = me & 1
    count = across_ref.shape[0]
    mine = pl.multiple_of(core * count, count)
    other = pl.multiple_of((core ^ 1) * count, count)
    x_ref[pl.ds(mine, count), :] = across_ref[...]
    x_ref[pl.ds(other, count), :] = beyond_ref[...]
    act_ref[...] = jnp.zeros_like(act_ref)
    back_ref[...] = jnp.zeros_like(back_ref)
    table = _read_table(table_ref)

    def grad(col):
        return grad_ref[:, col * blk : (col + 1) * blk]

    _term(blk, table, grad, weight_ref, lambda slot: None, x_ref, cot_ref, act_ref, back_ref)
    _write_rows(back_ref, other, count, send_ref)
    _write_rows(back_ref, mine, count, far_ref)


def _whole(
    blk,
    position_ref,
    live_ref,
    x_ref,
    grad_ref,
    wg_ref,
    wu_ref,
    cot_ref,
    term_ref,
    table_ref,
    weight_ref,
    act_ref,
    back_ref,
):
    weight_ref[:, :, :blk] = wg_ref[...]
    weight_ref[:, :, blk:] = wu_ref[...]
    act_ref[...] = jnp.zeros_like(act_ref)
    back_ref[...] = jnp.zeros_like(back_ref)
    _make_table(
        position_ref[...], live_ref[0, 0], cot_ref.shape[0] - 1, back_ref.shape[0], table_ref
    )
    table = _read_table(table_ref)

    def grad(col):
        return grad_ref[:, col * blk : (col + 1) * blk]

    _term(blk, table, grad, weight_ref, lambda slot: None, x_ref, cot_ref, act_ref, back_ref)
    _write_rows(back_ref, 0, x_ref.shape[0], term_ref)


def _weight_grads(blk, halves, table_ref, *refs):
    x_refs, cot_refs, (gate_ref, up_ref) = refs[:halves], refs[halves : 2 * halves], refs[-2:]
    for slot, (row, col) in enumerate(_read_table(table_ref)):
        start = pl.multiple_of(row * blk, blk)
        grads = lax.dot_general(
            jnp.concatenate([x_ref[:, pl.ds(start, blk)] for x_ref in x_refs], axis=0),
            jnp.concatenate([cot_ref[col] for cot_ref in cot_refs], axis=0),
            (((0,), (0,)), ((), ())),
            preferred_element_type=F32,
        )
        gate_ref[slot] = grads[:, :blk].astype(BF16)
        up_ref[slot] = grads[:, blk:].astype(BF16)


_pinned = pltpu.with_memory_space_constraint


def _swap(array, axis, distance):
    count = lax.axis_size(axis)
    return lax.ppermute(array, axis, [(i, i ^ distance) for i in range(count)])


def _params(mib):
    return pltpu.CompilerParams(vmem_limit_bytes=mib << 20)


def local(inputs, hidden_grad, top_grad, w_gate, w_up, block_pos, live_count):
    own_rows = inputs[0]
    count, width = own_rows.shape
    slots, blk = w_gate.shape[1], w_gate.shape[2]
    hidden = hidden_grad.shape[2]
    col_blocks, row_blocks = hidden // blk, width // blk
    tp = lax.axis_size("tp")
    sections = lax.axis_size("section")
    section = lax.axis_index("section")

    vmem = pl.BlockSpec(memory_space=pltpu.VMEM)
    smem = pl.BlockSpec(memory_space=pltpu.SMEM)
    hbm = pl.BlockSpec(memory_space=pltpu.HBM)
    struct = jax.ShapeDtypeStruct

    def cots(rows):
        return struct((col_blocks + 1, rows, 2 * blk), BF16)

    def sums(rows):
        return [
            pltpu.VMEM((col_blocks + 1, rows, 2 * blk), F32),
            pltpu.VMEM((row_blocks, rows, blk), F32),
        ]

    if tp == 4 and slots % PARTS == 0:
        rows = 2 * count
        across = _swap(own_rows, "tp", 2)
        beside = _swap(own_rows, "tp", 1)
        near_x, near_cot, keep, near_send, weights, far_grad, table = pl.pallas_call(
            functools.partial(_near_half, blk),
            out_shape=(
                struct((rows, width), BF16),
                cots(rows),
                struct((count, width), F32),
                struct((count, width), BF16),
                struct((slots, blk, 2 * blk), BF16),
                struct((rows, hidden), BF16),
                struct((2, slots), jnp.int32),
            ),
            in_specs=[hbm, smem, hbm, vmem, hbm, hbm, hbm],
            out_specs=[vmem] * 7,
            scratch_shapes=[
                pltpu.VMEM(block_pos.shape, jnp.int32),
                pltpu.VMEM((rows, hidden), BF16),
                *sums(rows),
                pltpu.SemaphoreType.DMA((4 + 2 * PARTS,)),
            ],
            compiler_params=_params(10),
            name="near_half",
        )(
            _pinned(block_pos, pltpu.HBM),
            live_count,
            _pinned(own_rows, pltpu.HBM),
            beside,
            *(_pinned(array[0], pltpu.HBM) for array in (hidden_grad, w_gate, w_up)),
        )
        across, near_send = lax.optimization_barrier((across, near_send))
        beyond = _swap(across, "tp", 1)
        far_x, far_cot, far, far_send = pl.pallas_call(
            functools.partial(_far_half, blk),
            out_shape=(
                struct((rows, width), BF16),
                cots(rows),
                struct((count, width), F32),
                struct((count, width), BF16),
            ),
            in_specs=[vmem] * 5,
            out_specs=[vmem] * 4,
            scratch_shapes=sums(rows),
            compiler_params=_params(10),
            name="far_half",
        )(table, across, beyond, far_grad, weights)
        near_came = _swap(near_send, "tp", 1)
        far_came = _swap(far_send, "tp", 1)
        crossed = _swap((far + far_came.astype(F32)).astype(BF16), "tp", 2)
        own_term = keep + near_came.astype(F32) + crossed.astype(F32)
        x_parts, cot_parts = (near_x, far_x), (near_cot, far_cot)
    else:
        rows = tp * count
        gathered = lax.all_gather(own_rows, "tp", axis=0, tiled=True)
        cot, term, table = pl.pallas_call(
            functools.partial(_whole, blk),
            out_shape=(cots(rows), struct((rows, width), BF16), struct((2, slots), jnp.int32)),
            in_specs=[vmem, smem] + [vmem] * 4,
            out_specs=[vmem] * 3,
            scratch_shapes=[pltpu.VMEM((slots, blk, 2 * blk), BF16), *sums(rows)],
            compiler_params=_params(24),
            name="whole",
        )(block_pos, live_count, gathered, hidden_grad[0], w_gate[0], w_up[0])
        own_term = lax.psum_scatter(term, "tp", scatter_dimension=0, tiled=True).astype(F32)
        x_parts, cot_parts = (gathered,), (cot,)

    gate_gradient, up_gradient = pl.pallas_call(
        functools.partial(_weight_grads, blk, len(x_parts)),
        out_shape=(struct((slots, blk, blk), BF16),) * 2,
        in_specs=[vmem] * (1 + 2 * len(x_parts)),
        out_specs=[vmem, vmem],
        compiler_params=_params(8),
        name="weight_grads",
    )(table, *x_parts, *cot_parts)

    total = own_term
    result = top_grad.astype(F32) + own_term
    if sections & (sections - 1) == 0:
        block = min(sections, 4)
        sent = own_term.astype(BF16)
        for step in range(1, block):
            other = _swap(sent, "section", step).astype(F32)
            result = result + jnp.where((section ^ step) > section, other, 0.0)
            total = total + other
        while block < sections:
            other = _swap(total.astype(BF16), "section", block ^ (block >> 1)).astype(F32)
            result = result + jnp.where(section & block == 0, other, 0.0)
            total = total + other
            block *= 2
    else:
        distance = 1
        while distance < sections:
            moves = [(i, i - distance) for i in range(distance, sections)]
            total = total + lax.ppermute(total.astype(BF16), "section", moves).astype(F32)
            distance *= 2
        result = top_grad.astype(F32) + total
    return (
        result.astype(BF16)[None],
        gate_gradient[None],
        up_gradient[None],
    )


def solution(mesh):
    in_specs = (
        P("section", "tp", None),
        P("section", None, "tp"),
        P("tp", None),
        P("section", "tp", None, None),
        P("section", "tp", None, None),
        P("section", "tp"),
        P("section", "tp"),
    )
    out_specs = (
        P("section", "tp", None),
        P("section", "tp", None, None),
        P("section", "tp", None, None),
    )
    return jax.shard_map(local, mesh=mesh, in_specs=in_specs, out_specs=out_specs, check_vma=False)
```

```python
import functools

import jax
import jax.numpy as jnp
from jax import lax
from jax.experimental import pallas as pl
from jax.experimental.pallas import tpu as pltpu
from jax.sharding import PartitionSpec as P

F32 = jnp.float32
BF16 = jnp.bfloat16
PARTS = 4


def _shift_and_factor(divisor, limit):
    for shift in range(31):
        factor = -(-(1 << shift) // divisor)
        if factor * limit < 1 << 31 and all(
            (p * factor) >> shift == p // divisor for p in range(limit)
        ):
            return factor, shift
    raise ValueError(divisor)


def _make_table(position, live, col_blocks, row_blocks, table_ref):
    factor, shift = _shift_and_factor(col_blocks, col_blocks * row_blocks)
    row = (position * factor) >> shift
    slot = lax.broadcasted_iota(jnp.int32, position.shape, 1)
    table_ref[0:1, :] = row
    table_ref[1:2, :] = jnp.where(slot < live, position - row * col_blocks, col_blocks)


def _read_table(table_ref):
    table = table_ref[...]
    return [(table[0, slot], table[1, slot]) for slot in range(table.shape[1])]


def _term(blk, table, grad, weight_ref, ready, x_ref, cot_ref, act_ref, back_ref):
    col_blocks = cot_ref.shape[0] - 1
    slots = len(table)
    for slot, (row, col) in enumerate(table):
        ready(slot)
        start = pl.multiple_of(row * blk, blk)
        act_ref[col] += jnp.dot(
            x_ref[:, pl.ds(start, blk)], weight_ref[slot], preferred_element_type=F32
        )
    for col in range(col_blocks):
        gate = act_ref[col, :, :blk]
        up = act_ref[col, :, blk:]
        upstream = grad(col).astype(F32)
        sig = jax.nn.sigmoid(gate)
        scaled = upstream * sig
        cot_ref[col, :, :blk] = (scaled * up * (1.0 + gate * (1.0 - sig))).astype(BF16)
        cot_ref[col, :, blk:] = (scaled * gate).astype(BF16)
    cot_ref[col_blocks] = jnp.zeros_like(cot_ref[col_blocks])
    for slot in range(slots):
        row, col = table[slot]
        back_ref[row] += lax.dot_general(
            cot_ref[col], weight_ref[slot], (((1,), (1,)), ((), ())), preferred_element_type=F32
        )


def _write_rows(back_ref, start, count, target):
    blk = back_ref.shape[2]
    for row in range(back_ref.shape[0]):
        target[:, row * blk : (row + 1) * blk] = back_ref[row, pl.ds(start, count), :].astype(
            target.dtype
        )


def _own_rows(
    blk,
    position_in,
    live_ref,
    own_in,
    grad_in,
    wg_in,
    wu_in,
    x_ref,
    cot_ref,
    term_ref,
    weight_ref,
    grad_ref,
    table_ref,
    position_ref,
    act_ref,
    back_ref,
    sems,
):
    slots = wg_in.shape[0]
    part = slots // PARTS
    position = pltpu.make_async_copy(position_in, position_ref, sems.at[2 * PARTS])
    own = pltpu.make_async_copy(own_in, x_ref, sems.at[2 * PARTS + 1])
    grads = pltpu.make_async_copy(grad_in, grad_ref, sems.at[2 * PARTS + 2])
    blocks = []
    for index in range(PARTS):
        span = pl.ds(index * part, part)
        blocks.append(
            [
                pltpu.make_async_copy(
                    wg_in.at[span], weight_ref.at[span, :, pl.ds(0, blk)], sems.at[2 * index]
                ),
                pltpu.make_async_copy(
                    wu_in.at[span], weight_ref.at[span, :, pl.ds(blk, blk)], sems.at[2 * index + 1]
                ),
            ]
        )
    for copy in (position, own, *sum(blocks, []), grads):
        copy.start()
    act_ref[...] = jnp.zeros_like(act_ref)
    back_ref[...] = jnp.zeros_like(back_ref)
    for copy in (position, own):
        copy.wait()
    _make_table(
        position_ref[...], live_ref[0, 0], cot_ref.shape[0] - 1, back_ref.shape[0], table_ref
    )

    def ready(slot):
        if slot % part == 0:
            for copy in blocks[slot // part]:
                copy.wait()

    grad = _grad_rows(grad_ref, 0, x_ref.shape[0], blk, grads.wait)
    _term(blk, _read_table(table_ref), grad, weight_ref, ready, x_ref, cot_ref, act_ref, back_ref)
    _write_rows(back_ref, 0, x_ref.shape[0], term_ref)


def _grad_rows(grad_ref, mask, count, blk, wait=None):
    start = pl.multiple_of((lax.axis_index("tp") ^ mask) * count, count)

    def grad(col):
        if col == 0 and wait is not None:
            wait()
        return grad_ref[pl.ds(start, count), col * blk : (col + 1) * blk]

    return grad


def _other_rows(
    blk, mask, table_ref, x_ref, grad_ref, weight_ref, cot_ref, term_ref, act_ref, back_ref
):
    count = x_ref.shape[0]
    act_ref[...] = jnp.zeros_like(act_ref)
    back_ref[...] = jnp.zeros_like(back_ref)
    grad = _grad_rows(grad_ref, mask, count, blk)
    table = _read_table(table_ref)
    _term(blk, table, grad, weight_ref, lambda slot: None, x_ref, cot_ref, act_ref, back_ref)
    _write_rows(back_ref, 0, count, term_ref)


def _whole(
    blk,
    position_ref,
    live_ref,
    x_ref,
    grad_ref,
    wg_ref,
    wu_ref,
    cot_ref,
    term_ref,
    table_ref,
    weight_ref,
    act_ref,
    back_ref,
):
    weight_ref[:, :, :blk] = wg_ref[...]
    weight_ref[:, :, blk:] = wu_ref[...]
    act_ref[...] = jnp.zeros_like(act_ref)
    back_ref[...] = jnp.zeros_like(back_ref)
    _make_table(
        position_ref[...], live_ref[0, 0], cot_ref.shape[0] - 1, back_ref.shape[0], table_ref
    )
    table = _read_table(table_ref)

    def grad(col):
        return grad_ref[:, col * blk : (col + 1) * blk]

    _term(blk, table, grad, weight_ref, lambda slot: None, x_ref, cot_ref, act_ref, back_ref)
    _write_rows(back_ref, 0, x_ref.shape[0], term_ref)


def _weight_grads(blk, halves, table_ref, *refs):
    x_refs, cot_refs, (gate_ref, up_ref) = refs[:halves], refs[halves : 2 * halves], refs[-2:]
    for slot, (row, col) in enumerate(_read_table(table_ref)):
        start = pl.multiple_of(row * blk, blk)
        grads = lax.dot_general(
            jnp.concatenate([x_ref[:, pl.ds(start, blk)] for x_ref in x_refs], axis=0),
            jnp.concatenate([cot_ref[col] for cot_ref in cot_refs], axis=0),
            (((0,), (0,)), ((), ())),
            preferred_element_type=F32,
        )
        gate_ref[slot] = grads[:, :blk].astype(BF16)
        up_ref[slot] = grads[:, blk:].astype(BF16)


_pinned = pltpu.with_memory_space_constraint


def _swap(array, axis, distance):
    count = lax.axis_size(axis)
    return lax.ppermute(array, axis, [(i, i ^ distance) for i in range(count)])


def _params(mib):
    return pltpu.CompilerParams(vmem_limit_bytes=mib << 20)


def local(inputs, hidden_grad, top_grad, w_gate, w_up, block_pos, live_count):
    own_rows = inputs[0]
    count, width = own_rows.shape
    slots, blk = w_gate.shape[1], w_gate.shape[2]
    hidden = hidden_grad.shape[2]
    col_blocks, row_blocks = hidden // blk, width // blk
    tp = lax.axis_size("tp")
    sections = lax.axis_size("section")
    section = lax.axis_index("section")

    vmem = pl.BlockSpec(memory_space=pltpu.VMEM)
    smem = pl.BlockSpec(memory_space=pltpu.SMEM)
    hbm = pl.BlockSpec(memory_space=pltpu.HBM)
    struct = jax.ShapeDtypeStruct

    def cots(rows):
        return struct((col_blocks + 1, rows, 2 * blk), BF16)

    def sums(rows):
        return [
            pltpu.VMEM((col_blocks + 1, rows, 2 * blk), F32),
            pltpu.VMEM((row_blocks, rows, blk), F32),
        ]

    if tp == 4 and slots % PARTS == 0:
        across = _swap(own_rows, "tp", 2)
        own_x, own_cot, keep, weights, grads, table = pl.pallas_call(
            functools.partial(_own_rows, blk),
            out_shape=(
                struct((count, width), BF16),
                cots(count),
                struct((count, width), F32),
                struct((slots, blk, 2 * blk), BF16),
                struct(hidden_grad.shape[1:], BF16),
                struct((2, slots), jnp.int32),
            ),
            in_specs=[hbm, smem, hbm, hbm, hbm, hbm],
            out_specs=[vmem] * 6,
            scratch_shapes=[
                pltpu.VMEM(block_pos.shape, jnp.int32),
                *sums(count),
                pltpu.SemaphoreType.DMA((2 * PARTS + 3,)),
            ],
            compiler_params=_params(10),
            name="own_rows",
        )(
            _pinned(block_pos, pltpu.HBM),
            live_count,
            _pinned(own_rows, pltpu.HBM),
            *(_pinned(array[0], pltpu.HBM) for array in (hidden_grad, w_gate, w_up)),
        )

        def others(mask, x, dtype, name):
            return pl.pallas_call(
                functools.partial(_other_rows, blk, mask),
                out_shape=(cots(count), struct((count, width), dtype)),
                in_specs=[vmem] * 4,
                out_specs=[vmem] * 2,
                scratch_shapes=sums(count),
                compiler_params=_params(10),
                name=name,
            )(table, x, grads, weights)

        beside = _swap(own_x, "tp", 1)
        across, keep = lax.optimization_barrier((across, keep))
        beyond = _swap(across, "tp", 1)
        across_cot, far = others(2, across, F32, "across_rows")
        beyond, far = lax.optimization_barrier((beyond, far))
        beyond_cot, far_send = others(3, beyond, BF16, "beyond_rows")
        far_came = _swap(far_send, "tp", 1)
        far = (far + far_came.astype(F32)).astype(BF16)
        far, beside = lax.optimization_barrier((far, beside))
        crossed = _swap(far, "tp", 2)
        beside_cot, near_send = others(1, beside, BF16, "beside_rows")
        near_came = _swap(near_send, "tp", 1)
        own_term = keep + near_came.astype(F32) + crossed.astype(F32)
        x_parts = own_x, beside, across, beyond
        cot_parts = own_cot, beside_cot, across_cot, beyond_cot
    else:
        rows = tp * count
        gathered = lax.all_gather(own_rows, "tp", axis=0, tiled=True)
        cot, term, table = pl.pallas_call(
            functools.partial(_whole, blk),
            out_shape=(cots(rows), struct((rows, width), BF16), struct((2, slots), jnp.int32)),
            in_specs=[vmem, smem] + [vmem] * 4,
            out_specs=[vmem] * 3,
            scratch_shapes=[pltpu.VMEM((slots, blk, 2 * blk), BF16), *sums(rows)],
            compiler_params=_params(24),
            name="whole",
        )(block_pos, live_count, gathered, hidden_grad[0], w_gate[0], w_up[0])
        own_term = lax.psum_scatter(term, "tp", scatter_dimension=0, tiled=True).astype(F32)
        x_parts, cot_parts = (gathered,), (cot,)

    gate_gradient, up_gradient = pl.pallas_call(
        functools.partial(_weight_grads, blk, len(x_parts)),
        out_shape=(struct((slots, blk, blk), BF16),) * 2,
        in_specs=[vmem] * (1 + 2 * len(x_parts)),
        out_specs=[vmem, vmem],
        compiler_params=_params(8),
        name="weight_grads",
    )(table, *x_parts, *cot_parts)

    total = own_term
    result = top_grad.astype(F32) + own_term
    if sections & (sections - 1) == 0:
        block = min(sections, 4)
        sent = own_term.astype(BF16)
        for step in range(1, block):
            other = _swap(sent, "section", step).astype(F32)
            result = result + jnp.where((section ^ step) > section, other, 0.0)
            total = total + other
        while block < sections:
            other = _swap(total.astype(BF16), "section", block ^ (block >> 1)).astype(F32)
            result = result + jnp.where(section & block == 0, other, 0.0)
            total = total + other
            block *= 2
    else:
        distance = 1
        while distance < sections:
            moves = [(i, i - distance) for i in range(distance, sections)]
            total = total + lax.ppermute(total.astype(BF16), "section", moves).astype(F32)
            distance *= 2
        result = top_grad.astype(F32) + total
    return (
        result.astype(BF16)[None],
        gate_gradient[None],
        up_gradient[None],
    )


def solution(mesh):
    in_specs = (
        P("section", "tp", None),
        P("section", None, "tp"),
        P("tp", None),
        P("section", "tp", None, None),
        P("section", "tp", None, None),
        P("section", "tp"),
        P("section", "tp"),
    )
    out_specs = (
        P("section", "tp", None),
        P("section", "tp", None, None),
        P("section", "tp", None, None),
    )
    return jax.shard_map(local, mesh=mesh, in_specs=in_specs, out_specs=out_specs, check_vma=False)
```

```python
import functools

import jax
import jax.numpy as jnp
from jax import lax
from jax.experimental import pallas as pl
from jax.experimental.pallas import tpu as pltpu
from jax.sharding import PartitionSpec as P

F32 = jnp.float32
BF16 = jnp.bfloat16
PARTS = 4


def _shift_and_factor(divisor, limit):
    for shift in range(31):
        factor = -(-(1 << shift) // divisor)
        if factor * limit < 1 << 31 and all(
            (p * factor) >> shift == p // divisor for p in range(limit)
        ):
            return factor, shift
    raise ValueError(divisor)


def _make_table(position, live, col_blocks, row_blocks, table_ref):
    factor, shift = _shift_and_factor(col_blocks, col_blocks * row_blocks)
    row = (position * factor) >> shift
    slot = lax.broadcasted_iota(jnp.int32, position.shape, 1)
    table_ref[0:1, :] = row
    table_ref[1:2, :] = jnp.where(slot < live, position - row * col_blocks, col_blocks)


def _read_table(table_ref):
    table = table_ref[...]
    return [(table[0, slot], table[1, slot]) for slot in range(table.shape[1])]


def _term(blk, table, grad, weight_ref, ready, x_ref, cot_ref, act_ref, back_ref):
    col_blocks = cot_ref.shape[0] - 1
    slots = len(table)
    for slot, (row, col) in enumerate(table):
        ready(slot)
        start = pl.multiple_of(row * blk, blk)
        act_ref[col] += jnp.dot(
            x_ref[:, pl.ds(start, blk)], weight_ref[slot], preferred_element_type=F32
        )
    for col in range(col_blocks):
        gate = act_ref[col, :, :blk]
        up = act_ref[col, :, blk:]
        upstream = grad(col).astype(F32)
        sig = jax.nn.sigmoid(gate)
        scaled = upstream * sig
        cot_ref[col, :, :blk] = (scaled * up * (1.0 + gate * (1.0 - sig))).astype(BF16)
        cot_ref[col, :, blk:] = (scaled * gate).astype(BF16)
    cot_ref[col_blocks] = jnp.zeros_like(cot_ref[col_blocks])
    for slot in range(slots):
        row, col = table[slot]
        back_ref[row] += lax.dot_general(
            cot_ref[col], weight_ref[slot], (((1,), (1,)), ((), ())), preferred_element_type=F32
        )


def _write_rows(back_ref, start, count, target):
    blk = back_ref.shape[2]
    for row in range(back_ref.shape[0]):
        target[:, row * blk : (row + 1) * blk] = back_ref[row, pl.ds(start, count), :].astype(
            target.dtype
        )


def _own_rows(
    blk,
    position_in,
    live_ref,
    own_in,
    grad_in,
    wg_in,
    wu_in,
    x_ref,
    cot_ref,
    term_ref,
    weight_ref,
    grad_ref,
    table_ref,
    position_ref,
    act_ref,
    back_ref,
    sems,
):
    slots = wg_in.shape[0]
    part = slots // PARTS
    position = pltpu.make_async_copy(position_in, position_ref, sems.at[2 * PARTS])
    own = pltpu.make_async_copy(own_in, x_ref, sems.at[2 * PARTS + 1])
    grads = pltpu.make_async_copy(grad_in, grad_ref, sems.at[2 * PARTS + 2])
    blocks = []
    for index in range(PARTS):
        span = pl.ds(index * part, part)
        blocks.append(
            [
                pltpu.make_async_copy(
                    wg_in.at[span], weight_ref.at[span, :, pl.ds(0, blk)], sems.at[2 * index]
                ),
                pltpu.make_async_copy(
                    wu_in.at[span], weight_ref.at[span, :, pl.ds(blk, blk)], sems.at[2 * index + 1]
                ),
            ]
        )
    for copy in (position, own, *sum(blocks, []), grads):
        copy.start()
    act_ref[...] = jnp.zeros_like(act_ref)
    back_ref[...] = jnp.zeros_like(back_ref)
    for copy in (position, own):
        copy.wait()
    _make_table(
        position_ref[...], live_ref[0, 0], cot_ref.shape[0] - 1, back_ref.shape[0], table_ref
    )

    def ready(slot):
        if slot % part == 0:
            for copy in blocks[slot // part]:
                copy.wait()

    grad = _grad_rows(grad_ref, 0, x_ref.shape[0], blk, grads.wait)
    _term(blk, _read_table(table_ref), grad, weight_ref, ready, x_ref, cot_ref, act_ref, back_ref)
    _write_rows(back_ref, 0, x_ref.shape[0], term_ref)


def _grad_rows(grad_ref, mask, count, blk, wait=None):
    start = pl.multiple_of((lax.axis_index("tp") ^ mask) * count, count)

    def grad(col):
        if col == 0 and wait is not None:
            wait()
        return grad_ref[pl.ds(start, count), col * blk : (col + 1) * blk]

    return grad


def _other_rows(
    blk, mask, table_ref, x_ref, grad_ref, weight_ref, cot_ref, term_ref, act_ref, back_ref
):
    count = x_ref.shape[0]
    act_ref[...] = jnp.zeros_like(act_ref)
    back_ref[...] = jnp.zeros_like(back_ref)
    grad = _grad_rows(grad_ref, mask, count, blk)
    table = _read_table(table_ref)
    _term(blk, table, grad, weight_ref, lambda slot: None, x_ref, cot_ref, act_ref, back_ref)
    _write_rows(back_ref, 0, count, term_ref)


def _whole(
    blk,
    position_ref,
    live_ref,
    x_ref,
    grad_ref,
    wg_ref,
    wu_ref,
    cot_ref,
    term_ref,
    table_ref,
    weight_ref,
    act_ref,
    back_ref,
):
    weight_ref[:, :, :blk] = wg_ref[...]
    weight_ref[:, :, blk:] = wu_ref[...]
    act_ref[...] = jnp.zeros_like(act_ref)
    back_ref[...] = jnp.zeros_like(back_ref)
    _make_table(
        position_ref[...], live_ref[0, 0], cot_ref.shape[0] - 1, back_ref.shape[0], table_ref
    )
    table = _read_table(table_ref)

    def grad(col):
        return grad_ref[:, col * blk : (col + 1) * blk]

    _term(blk, table, grad, weight_ref, lambda slot: None, x_ref, cot_ref, act_ref, back_ref)
    _write_rows(back_ref, 0, x_ref.shape[0], term_ref)


def _weight_grads(blk, halves, table_ref, *refs):
    x_refs, cot_refs, (gate_ref, up_ref) = refs[:halves], refs[halves : 2 * halves], refs[-2:]
    for slot, (row, col) in enumerate(_read_table(table_ref)):
        start = pl.multiple_of(row * blk, blk)
        grads = lax.dot_general(
            jnp.concatenate([x_ref[:, pl.ds(start, blk)] for x_ref in x_refs], axis=0),
            jnp.concatenate([cot_ref[col] for cot_ref in cot_refs], axis=0),
            (((0,), (0,)), ((), ())),
            preferred_element_type=F32,
        )
        gate_ref[slot] = grads[:, :blk].astype(BF16)
        up_ref[slot] = grads[:, blk:].astype(BF16)


_pinned = pltpu.with_memory_space_constraint


def _swap(array, axis, distance):
    count = lax.axis_size(axis)
    return lax.ppermute(array, axis, [(i, i ^ distance) for i in range(count)])


def _params(mib):
    return pltpu.CompilerParams(vmem_limit_bytes=mib << 20)


def local(inputs, hidden_grad, top_grad, w_gate, w_up, block_pos, live_count):
    own_rows = inputs[0]
    count, width = own_rows.shape
    slots, blk = w_gate.shape[1], w_gate.shape[2]
    hidden = hidden_grad.shape[2]
    col_blocks, row_blocks = hidden // blk, width // blk
    tp = lax.axis_size("tp")
    sections = lax.axis_size("section")
    section = lax.axis_index("section")

    vmem = pl.BlockSpec(memory_space=pltpu.VMEM)
    smem = pl.BlockSpec(memory_space=pltpu.SMEM)
    hbm = pl.BlockSpec(memory_space=pltpu.HBM)
    struct = jax.ShapeDtypeStruct

    def cots(rows):
        return struct((col_blocks + 1, rows, 2 * blk), BF16)

    def sums(rows):
        return [
            pltpu.VMEM((col_blocks + 1, rows, 2 * blk), F32),
            pltpu.VMEM((row_blocks, rows, blk), F32),
        ]

    if tp == 4 and slots % PARTS == 0:
        across = _swap(own_rows, "tp", 2)
        own_x, own_cot, keep, weights, grads, table = pl.pallas_call(
            functools.partial(_own_rows, blk),
            out_shape=(
                struct((count, width), BF16),
                cots(count),
                struct((count, width), F32),
                struct((slots, blk, 2 * blk), BF16),
                struct(hidden_grad.shape[1:], BF16),
                struct((2, slots), jnp.int32),
            ),
            in_specs=[hbm, smem, hbm, hbm, hbm, hbm],
            out_specs=[vmem] * 6,
            scratch_shapes=[
                pltpu.VMEM(block_pos.shape, jnp.int32),
                *sums(count),
                pltpu.SemaphoreType.DMA((2 * PARTS + 3,)),
            ],
            compiler_params=_params(10),
            name="own_rows",
        )(
            _pinned(block_pos, pltpu.HBM),
            live_count,
            _pinned(own_rows, pltpu.HBM),
            *(_pinned(array[0], pltpu.HBM) for array in (hidden_grad, w_gate, w_up)),
        )

        def others(mask, x, dtype, name):
            return pl.pallas_call(
                functools.partial(_other_rows, blk, mask),
                out_shape=(cots(count), struct((count, width), dtype)),
                in_specs=[vmem] * 4,
                out_specs=[vmem] * 2,
                scratch_shapes=sums(count),
                compiler_params=_params(10),
                name=name,
            )(table, x, grads, weights)

        beside = _swap(own_x, "tp", 1)
        across, keep = lax.optimization_barrier((across, keep))
        beyond = _swap(across, "tp", 1)
        across_cot, far = others(2, across, F32, "across_rows")
        beyond, far, beside = lax.optimization_barrier((beyond, far, beside))
        beyond_cot, far_send = others(3, beyond, BF16, "beyond_rows")
        beside_cot, near_send = others(1, beside, BF16, "beside_rows")
        far_came = _swap(far_send, "tp", 1)
        far_came, near_send = lax.optimization_barrier((far_came, near_send))
        far = (far + far_came.astype(F32)).astype(BF16)
        crossed = _swap(far, "tp", 2)
        near_came = _swap(near_send, "tp", 1)
        own_term = keep + near_came.astype(F32) + crossed.astype(F32)
        x_parts = own_x, beside, across, beyond
        cot_parts = own_cot, beside_cot, across_cot, beyond_cot
    else:
        rows = tp * count
        gathered = lax.all_gather(own_rows, "tp", axis=0, tiled=True)
        cot, term, table = pl.pallas_call(
            functools.partial(_whole, blk),
            out_shape=(cots(rows), struct((rows, width), BF16), struct((2, slots), jnp.int32)),
            in_specs=[vmem, smem] + [vmem] * 4,
            out_specs=[vmem] * 3,
            scratch_shapes=[pltpu.VMEM((slots, blk, 2 * blk), BF16), *sums(rows)],
            compiler_params=_params(24),
            name="whole",
        )(block_pos, live_count, gathered, hidden_grad[0], w_gate[0], w_up[0])
        own_term = lax.psum_scatter(term, "tp", scatter_dimension=0, tiled=True).astype(F32)
        x_parts, cot_parts = (gathered,), (cot,)

    gate_gradient, up_gradient = pl.pallas_call(
        functools.partial(_weight_grads, blk, len(x_parts)),
        out_shape=(struct((slots, blk, blk), BF16),) * 2,
        in_specs=[vmem] * (1 + 2 * len(x_parts)),
        out_specs=[vmem, vmem],
        compiler_params=_params(8),
        name="weight_grads",
    )(table, *x_parts, *cot_parts)

    total = own_term
    result = top_grad.astype(F32) + own_term
    if sections & (sections - 1) == 0:
        block = min(sections, 4)
        sent = own_term.astype(BF16)
        for step in range(1, block):
            other = _swap(sent, "section", step).astype(F32)
            result = result + jnp.where((section ^ step) > section, other, 0.0)
            total = total + other
        while block < sections:
            other = _swap(total.astype(BF16), "section", block ^ (block >> 1)).astype(F32)
            result = result + jnp.where(section & block == 0, other, 0.0)
            total = total + other
            block *= 2
    else:
        distance = 1
        while distance < sections:
            moves = [(i, i - distance) for i in range(distance, sections)]
            total = total + lax.ppermute(total.astype(BF16), "section", moves).astype(F32)
            distance *= 2
        result = top_grad.astype(F32) + total
    return (
        result.astype(BF16)[None],
        gate_gradient[None],
        up_gradient[None],
    )


def solution(mesh):
    in_specs = (
        P("section", "tp", None),
        P("section", None, "tp"),
        P("tp", None),
        P("section", "tp", None, None),
        P("section", "tp", None, None),
        P("section", "tp"),
        P("section", "tp"),
    )
    out_specs = (
        P("section", "tp", None),
        P("section", "tp", None, None),
        P("section", "tp", None, None),
    )
    return jax.shard_map(local, mesh=mesh, in_specs=in_specs, out_specs=out_specs, check_vma=False)
```

```python
import functools

import jax
import jax.numpy as jnp
from jax import lax
from jax.experimental import pallas as pl
from jax.experimental.pallas import tpu as pltpu
from jax.sharding import PartitionSpec as P

F32 = jnp.float32
BF16 = jnp.bfloat16


def _shift_and_factor(divisor, limit):
    for shift in range(31):
        factor = -(-(1 << shift) // divisor)
        if factor * limit < 1 << 31 and all(
            (p * factor) >> shift == p // divisor for p in range(limit)
        ):
            return factor, shift
    raise ValueError(divisor)


def _make_table(position, live, col_blocks, row_blocks, table_ref):
    factor, shift = _shift_and_factor(col_blocks, col_blocks * row_blocks)
    row = (position * factor) >> shift
    slot = lax.broadcasted_iota(jnp.int32, position.shape, 1)
    table_ref[0:1, :] = row
    table_ref[1:2, :] = jnp.where(slot < live, position - row * col_blocks, col_blocks)


def _read_table(table_ref):
    table = table_ref[...]
    return [(table[0, slot], table[1, slot]) for slot in range(table.shape[1])]


def _cotangents(blk, table, grad, weight, x_ref, cot_ref, act_ref):
    col_blocks = cot_ref.shape[0] - 1
    act_ref[...] = jnp.zeros_like(act_ref)
    for slot, (row, col) in enumerate(table):
        start = pl.multiple_of(row * blk, blk)
        act_ref[col] += jnp.dot(
            x_ref[:, pl.ds(start, blk)], weight(slot), preferred_element_type=F32
        )
    for col in range(col_blocks):
        gate = act_ref[col, :, :blk]
        up = act_ref[col, :, blk:]
        upstream = grad(col).astype(F32)
        sig = jax.nn.sigmoid(gate)
        scaled = upstream * sig
        cot_ref[col, :, :blk] = (scaled * up * (1.0 + gate * (1.0 - sig))).astype(BF16)
        cot_ref[col, :, blk:] = (scaled * gate).astype(BF16)
    cot_ref[col_blocks] = jnp.zeros_like(cot_ref[col_blocks])


def _add_back(table, weight, cot_ref, back_ref):
    for slot, (row, col) in enumerate(table):
        back_ref[row] += lax.dot_general(
            cot_ref[col], weight(slot), (((1,), (1,)), ((), ())), preferred_element_type=F32
        )


def _beside(gate_ref, up_ref):
    return lambda slot: jnp.concatenate([gate_ref[slot], up_ref[slot]], axis=1)


def _write_rows(back_ref, start, count, target):
    blk = back_ref.shape[2]
    for row in range(back_ref.shape[0]):
        target[:, row * blk : (row + 1) * blk] = back_ref[row, pl.ds(start, count), :].astype(
            target.dtype
        )


def _stage(
    col_blocks,
    row_blocks,
    position_in,
    live_ref,
    own_in,
    grad_in,
    wg_in,
    wu_in,
    x_ref,
    weight_ref,
    grad_ref,
    table_ref,
    position_ref,
    sems,
):
    blk = wg_in.shape[2]
    position = pltpu.make_async_copy(position_in, position_ref, sems.at[0])
    copies = [
        pltpu.make_async_copy(wg_in, weight_ref.at[:, :, pl.ds(0, blk)], sems.at[1]),
        pltpu.make_async_copy(wu_in, weight_ref.at[:, :, pl.ds(blk, blk)], sems.at[2]),
        pltpu.make_async_copy(grad_in, grad_ref, sems.at[3]),
        pltpu.make_async_copy(own_in, x_ref, sems.at[4]),
    ]
    for copy in (position, *copies):
        copy.start()
    position.wait()
    _make_table(position_ref[...], live_ref[0, 0], col_blocks, row_blocks, table_ref)
    for copy in copies:
        copy.wait()


def _grad_rows(grad_ref, mask, count, blk):
    start = pl.multiple_of((lax.axis_index("tp") ^ mask) * count, count)

    def grad(col):
        return grad_ref[pl.ds(start, count), col * blk : (col + 1) * blk]

    return grad


def _across_rows(
    blk, table_ref, x_ref, grad_ref, weight_ref, cot_ref, back_ref, act_ref
):
    back_ref[...] = jnp.zeros_like(back_ref)
    table = _read_table(table_ref)

    def weight(slot):
        return weight_ref[slot]

    grad = _grad_rows(grad_ref, 2, x_ref.shape[0], blk)
    _cotangents(blk, table, grad, weight, x_ref, cot_ref, act_ref)
    _add_back(table, weight, cot_ref, back_ref)


def _across_other(
    blk, table_ref, x_ref, grad_ref, wg_ref, wu_ref, in_ref, term_ref, cot_ref, act_ref, back_ref
):
    back_ref[...] = in_ref[...]
    count = x_ref.shape[0]
    table, weight = _read_table(table_ref), _beside(wg_ref, wu_ref)
    _cotangents(
        blk, table, _grad_rows(grad_ref, 2, count, blk), weight, x_ref, cot_ref, act_ref
    )
    _add_back(table, weight, cot_ref, back_ref)
    _write_rows(back_ref, 0, count, term_ref)


def _own_rows(
    blk,
    table_ref,
    x_ref,
    grad_ref,
    weight_ref,
    other_table_ref,
    other_grad_ref,
    other_wg_ref,
    other_wu_ref,
    cot_ref,
    term_ref,
    other_cot_ref,
    act_ref,
    other_act_ref,
    back_ref,
):
    count = x_ref.shape[0]
    back_ref[...] = jnp.zeros_like(back_ref)
    table, other_table = _read_table(table_ref), _read_table(other_table_ref)
    grad = _grad_rows(grad_ref, 0, count, blk)
    other_grad = _grad_rows(other_grad_ref, 0, count, blk)
    other_weight = _beside(other_wg_ref, other_wu_ref)

    def weight(slot):
        return weight_ref[slot]

    _cotangents(blk, table, grad, weight, x_ref, cot_ref, act_ref)
    _cotangents(blk, other_table, other_grad, other_weight, x_ref, other_cot_ref, other_act_ref)
    _add_back(table, weight, cot_ref, back_ref)
    _add_back(other_table, other_weight, other_cot_ref, back_ref)
    _write_rows(back_ref, 0, count, term_ref)


def _rest_rows(
    blk, table_ref, beside_ref, beyond_ref, grad_ref, weight_ref, cot_ref, far_cot_ref, act_ref
):
    count = beside_ref.shape[0]
    table = _read_table(table_ref)

    def weight(slot):
        return weight_ref[slot]

    for mask, x_ref, out_ref in ((1, beside_ref, cot_ref), (3, beyond_ref, far_cot_ref)):
        grad = _grad_rows(grad_ref, mask, count, blk)
        _cotangents(blk, table, grad, weight, x_ref, out_ref, act_ref)


def _whole(
    blk,
    position_ref,
    live_ref,
    x_ref,
    grad_ref,
    wg_ref,
    wu_ref,
    cot_ref,
    term_ref,
    table_ref,
    weight_ref,
    act_ref,
    back_ref,
):
    weight_ref[:, :, :blk] = wg_ref[...]
    weight_ref[:, :, blk:] = wu_ref[...]
    back_ref[...] = jnp.zeros_like(back_ref)
    _make_table(
        position_ref[...], live_ref[0, 0], cot_ref.shape[0] - 1, back_ref.shape[0], table_ref
    )
    table = _read_table(table_ref)

    def grad(col):
        return grad_ref[:, col * blk : (col + 1) * blk]

    def weight(slot):
        return weight_ref[slot]

    _cotangents(blk, table, grad, weight, x_ref, cot_ref, act_ref)
    _add_back(table, weight, cot_ref, back_ref)
    _write_rows(back_ref, 0, x_ref.shape[0], term_ref)


def _weight_grads(blk, halves, table_ref, *refs):
    x_refs, cot_refs, (gate_ref, up_ref) = refs[:halves], refs[halves : 2 * halves], refs[-2:]
    for slot, (row, col) in enumerate(_read_table(table_ref)):
        start = pl.multiple_of(row * blk, blk)
        grads = lax.dot_general(
            jnp.concatenate([x_ref[:, pl.ds(start, blk)] for x_ref in x_refs], axis=0),
            jnp.concatenate([cot_ref[col] for cot_ref in cot_refs], axis=0),
            (((0,), (0,)), ((), ())),
            preferred_element_type=F32,
        )
        gate_ref[slot] = grads[:, :blk].astype(BF16)
        up_ref[slot] = grads[:, blk:].astype(BF16)


_pinned = pltpu.with_memory_space_constraint


def _swap(array, axis, distance):
    count = lax.axis_size(axis)
    return lax.ppermute(array, axis, [(i, i ^ distance) for i in range(count)])


def _params(mib):
    return pltpu.CompilerParams(vmem_limit_bytes=mib << 20)


def local(inputs, hidden_grad, top_grad, w_gate, w_up, block_pos, live_count):
    own_rows = inputs[0]
    count, width = own_rows.shape
    slots, blk = w_gate.shape[1], w_gate.shape[2]
    hidden = hidden_grad.shape[2]
    col_blocks, row_blocks = hidden // blk, width // blk
    tp = lax.axis_size("tp")
    sections = lax.axis_size("section")
    section = lax.axis_index("section")

    vmem = pl.BlockSpec(memory_space=pltpu.VMEM)
    smem = pl.BlockSpec(memory_space=pltpu.SMEM)
    hbm = pl.BlockSpec(memory_space=pltpu.HBM)
    struct = jax.ShapeDtypeStruct

    def cots(rows):
        return struct((col_blocks + 1, rows, 2 * blk), BF16)

    def sums(rows):
        return [
            pltpu.VMEM((col_blocks + 1, rows, 2 * blk), F32),
            pltpu.VMEM((row_blocks, rows, blk), F32),
        ]

    if tp == 4:
        across = _swap(own_rows, "tp", 2)
        own_x, weights, grads, table = pl.pallas_call(
            functools.partial(_stage, col_blocks, row_blocks),
            out_shape=(
                struct((count, width), BF16),
                struct((slots, blk, 2 * blk), BF16),
                struct(hidden_grad.shape[1:], BF16),
                struct((2, slots), jnp.int32),
            ),
            in_specs=[hbm, smem, hbm, hbm, hbm, hbm],
            out_specs=[vmem] * 4,
            scratch_shapes=[
                pltpu.VMEM(block_pos.shape, jnp.int32),
                pltpu.SemaphoreType.DMA((5,)),
            ],
            compiler_params=_params(4),
            name="stage",
            cost_estimate=pl.CostEstimate(flops=1150000, transcendentals=0, bytes_accessed=0),
        )(
            _pinned(block_pos, pltpu.HBM),
            live_count,
            _pinned(own_rows, pltpu.HBM),
            *(_pinned(array[0], pltpu.HBM) for array in (hidden_grad, w_gate, w_up)),
        )
        other_wg, other_wu, other_grads, other_table = (
            _swap(array, "tp", 1) for array in (w_gate[0], w_up[0], hidden_grad[0], table)
        )
        across, own_x = lax.optimization_barrier((across, own_x))
        act, back = sums(count)
        across_cot, far = pl.pallas_call(
            functools.partial(_across_rows, blk),
            out_shape=(cots(count), struct((row_blocks, count, blk), F32)),
            in_specs=[vmem] * 4,
            out_specs=[vmem] * 2,
            scratch_shapes=[act],
            compiler_params=_params(4),
            name="across_rows",
            cost_estimate=pl.CostEstimate(flops=13800000000, transcendentals=0, bytes_accessed=0),
        )(table, across, grads, weights)
        other_wg, other_wu, other_grads, far = lax.optimization_barrier(
            (other_wg, other_wu, other_grads, far)
        )
        far = pl.pallas_call(
            functools.partial(_across_other, blk),
            out_shape=struct((count, width), BF16),
            in_specs=[vmem] * 6,
            out_specs=vmem,
            scratch_shapes=[pltpu.VMEM(cots(count).shape, BF16), act, back],
            compiler_params=_params(4),
            name="across_other",
        )(other_table, across, other_grads, other_wg, other_wu, far)
        far, own_late, across_late = lax.optimization_barrier((far, own_x, across))
        crossed = _swap(far, "tp", 2)
        own_cot, keep = pl.pallas_call(
            functools.partial(_own_rows, blk),
            out_shape=(cots(count), struct((count, width), F32)),
            in_specs=[vmem] * 8,
            out_specs=[vmem] * 2,
            scratch_shapes=[pltpu.VMEM(cots(count).shape, BF16), act, act, back],
            compiler_params=_params(4),
            name="own_rows",
        )(table, own_late, grads, weights, other_table, other_grads, other_wg, other_wu)
        beside = _swap(own_late, "tp", 1)
        beyond = _swap(across_late, "tp", 1)
        beside_cot, beyond_cot = pl.pallas_call(
            functools.partial(_rest_rows, blk),
            out_shape=(cots(count),) * 2,
            in_specs=[vmem] * 5,
            out_specs=[vmem] * 2,
            scratch_shapes=[act],
            compiler_params=_params(4),
            name="rest_rows",
        )(table, beside, beyond, grads, weights)
        own_term = keep + crossed.astype(F32)
        x_parts = own_late, beside, across_late, beyond
        cot_parts = own_cot, beside_cot, across_cot, beyond_cot
    else:
        rows = tp * count
        gathered = lax.all_gather(own_rows, "tp", axis=0, tiled=True)
        cot, term, table = pl.pallas_call(
            functools.partial(_whole, blk),
            out_shape=(cots(rows), struct((rows, width), BF16), struct((2, slots), jnp.int32)),
            in_specs=[vmem, smem] + [vmem] * 4,
            out_specs=[vmem] * 3,
            scratch_shapes=[pltpu.VMEM((slots, blk, 2 * blk), BF16), *sums(rows)],
            compiler_params=_params(24),
            name="whole",
        )(block_pos, live_count, gathered, hidden_grad[0], w_gate[0], w_up[0])
        own_term = lax.psum_scatter(term, "tp", scatter_dimension=0, tiled=True).astype(F32)
        x_parts, cot_parts = (gathered,), (cot,)

    total = own_term
    result = top_grad.astype(F32) + own_term
    if sections & (sections - 1) == 0:
        block = min(sections, 4)
        sent = own_term.astype(BF16)
        for step in range(1, block):
            other = _swap(sent, "section", step).astype(F32)
            result = result + jnp.where((section ^ step) > section, other, 0.0)
            total = total + other
        if tp == 4:
            total, *cot_parts = lax.optimization_barrier((total, *cot_parts))
        while block < sections:
            other = _swap(total.astype(BF16), "section", block ^ (block >> 1)).astype(F32)
            result = result + jnp.where(section & block == 0, other, 0.0)
            total = total + other
            block *= 2
    else:
        distance = 1
        while distance < sections:
            moves = [(i, i - distance) for i in range(distance, sections)]
            total = total + lax.ppermute(total.astype(BF16), "section", moves).astype(F32)
            distance *= 2
        result = top_grad.astype(F32) + total
    gate_gradient, up_gradient = pl.pallas_call(
        functools.partial(_weight_grads, blk, len(x_parts)),
        out_shape=(struct((slots, blk, blk), BF16),) * 2,
        in_specs=[vmem] * (1 + 2 * len(x_parts)),
        out_specs=[vmem, vmem],
        compiler_params=_params(4),
        name="weight_grads",
    )(table, *x_parts, *cot_parts)

    return (
        result.astype(BF16)[None],
        gate_gradient[None],
        up_gradient[None],
    )


def solution(mesh):
    in_specs = (
        P("section", "tp", None),
        P("section", None, "tp"),
        P("tp", None),
        P("section", "tp", None, None),
        P("section", "tp", None, None),
        P("section", "tp"),
        P("section", "tp"),
    )
    out_specs = (
        P("section", "tp", None),
        P("section", "tp", None, None),
        P("section", "tp", None, None),
    )
    return jax.shard_map(local, mesh=mesh, in_specs=in_specs, out_specs=out_specs, check_vma=False)
```
